32 devices in a mesh: groups: 2 (over x), tok: 16 (over z, y, core).
Axes of the slice: x: 2, y: 2, z: 4, core: 2. Of those that a mesh axis runs over, the one named last changes fastest.
Arguments:
- query_tokens: bfloat16 [3, 4096, 1024], P(None, ('groups', 'tok')), parts along dimension 1, may hold values from -6 to 6
- key_tokens: bfloat16 [3, 4096, 1024], P(None, ('groups', 'tok')), parts along dimension 1, may hold values from -6 to 6
- value_tokens: bfloat16 [3, 4096, 1024], P(None, ('groups', 'tok')), parts along dimension 1, may hold values from -6 to 6
- learn_rates: float32 [3, 4096, 2], P(None, ('groups', 'tok')), parts along dimension 1, may hold values from 0.0009765625 to 0.00390625
- fast_first: bfloat16 [2, 512, 512], P(None, 'tok'), may hold values from -0.25 to 0.25
- fast_third: bfloat16 [2, 512, 512], P(None, 'tok'), may hold values from -0.25 to 0.25
- fast_second: bfloat16 [2, 512, 512], P(None, 'tok'), may hold values from -0.25 to 0.25
- momentum_decay: float32 [2], replicated, may hold values from 0.3 to 0.95
Outputs:
- readout: bfloat16 [3, 4096, 1024], P(None, ('groups', 'tok')), parts along dimension 1
The draws below stay inside these ranges and needn't reach their ends.
There are 2 independent parts, one for each index of `groups`. The reference program is written for one: setup_inputs(seed, part) draws one part's arguments, and reference() takes and returns one part's arrays. A program takes and returns all parts, laid end to end along the dimension named above; an argument that names none is the same for every part. Nothing has to cross between parts.
All inputs are finite; a program needn't handle non-finite values.
Results may differ from the reference program's by a relative error of at most 0.0089.
Values may be sent and summed in bfloat16 or wider, within the bound.
A program may use at most 64 MiB of HBM per device.

```python
import math
import jax
import jax.numpy as jnp
from jax import lax

HEADS = 2
HD = 512
FH = 512
NCHUNK = 3
TOK_DEV = 128
CH = 2048


def raised(array, key, source, target, parts, factor):
    owner, partner = [(jnp.arange(array.shape[axis_at]) // (array.shape[axis_at] // parts)).reshape([-1 if axis == axis_at else 1 for axis in range(array.ndim)]) for axis_at in (source, target)]
    chosen = jax.random.permutation(key, parts)[partner]
    strong = (owner == chosen) | (owner == (partner + parts // 2) % parts)
    return jnp.where(strong, factor * array, array)


def block_scale(key, dims, cuts, least, largest):
    gain = 1.0
    for dim, parts in cuts:
        steps = jax.random.uniform(jax.random.fold_in(jax.random.fold_in(key, 6), dim), (parts,), jnp.float32, least / len(cuts), largest / len(cuts))
        gain = gain * jnp.repeat(jnp.exp(steps), dims[dim] // parts).reshape((-1,) + (1,) * (len(dims) - 1 - dim))
    return gain


def centred(stream_key, extent, scale, most, cuts=(), kind=jnp.bfloat16):
    values = jax.random.normal(stream_key, extent, jnp.float32) * scale
    if len(cuts) > 0:
        values = block_scale(stream_key, extent, cuts, -0.22, 0.18) * values
    return jnp.clip(values, min=-most, max=most).astype(kind)


def bell_draw_with(key, shape, spread, reach, shards, heavy, kind=jnp.bfloat16):
    values = spread * jax.random.normal(key, shape, jnp.float32)
    if shards:
        values = values * block_scale(key, shape, shards, -0.22, 0.18)
    return jnp.clip(raised(values, jax.random.fold_in(key, 3), *heavy), -reach, reach).astype(kind)


def setup_inputs(seed: int = 0, part: int = 0) -> dict:
    seeds = jax.random.split(jax.random.key(seed), 9)
    own_keys = jax.random.split(jax.random.fold_in(seeds[8], part), 9)
    return {
        "query_tokens": centred(own_keys[0], (NCHUNK, CH, HEADS * HD), 1.0, 6.0, ((1, 16),)),
        "key_tokens": centred(own_keys[1], (NCHUNK, CH, HEADS * HD), 1.0, 6.0, ((1, 16),)),
        "value_tokens": bell_draw_with(own_keys[2], (NCHUNK, CH, HEADS * HD), 1.0, 6.0, ((1, 16),), (1, 2, 16, 2.0)),
        "learn_rates": jnp.clip(jnp.exp(math.log(0.00390625) - 1.3862944 * jax.random.uniform(own_keys[3], (NCHUNK, CH, HEADS), jnp.float32) ** block_scale(own_keys[3], (NCHUNK, CH, HEADS), ((1, 16),), -0.2, 0.2)), 0.0009765625, 0.00390625),
        "fast_first": centred(seeds[4], (HEADS, FH, HD), HD ** -0.5, 0.25, ((1, 16),)),
        "fast_third": centred(seeds[5], (HEADS, FH, HD), HD ** -0.5, 0.25, ((1, 16),)),
        "fast_second": centred(seeds[6], (HEADS, HD, FH), FH ** -0.5, 0.25, ((1, 16),)),
        "momentum_decay": jnp.clip(jax.random.uniform(seeds[7], (HEADS,), jnp.float32, 0.3, 0.95), 0.3, 0.95),
    }


def forward_parts(weights, inputs):
    first, third, second = weights
    length = inputs.shape[0]
    head_count = first.shape[0]
    shaped = inputs.reshape(length, head_count, -1).astype(jnp.float32)
    pre_gate = jnp.einsum('thd,hfd->htf', shaped, first.astype(jnp.float32))
    pre_up = jnp.einsum('thd,hfd->htf', shaped, third.astype(jnp.float32))
    hidden = (jax.nn.silu(pre_gate) * pre_up).astype(jnp.bfloat16)
    return (shaped, pre_gate, pre_up, hidden)

def apply_block(weights, inputs):
    shaped, pre_gate, pre_up, hidden = forward_parts(weights, inputs)
    result = jnp.einsum('htf,hdf->thd', hidden.astype(jnp.float32), weights[2].astype(jnp.float32))
    return result.reshape(inputs.shape[0], -1)

def apply_all(weights, inputs):
    blocks = inputs.reshape(CH // TOK_DEV, TOK_DEV, inputs.shape[1])
    result = lax.map(lambda piece: apply_block(weights, piece), blocks)
    return result.reshape(CH, inputs.shape[1])

def step_block(weights, keys, values, rates):
    shaped, pre_gate, pre_up, hidden = forward_parts(weights, keys)
    length = keys.shape[0]
    head_count = weights[0].shape[0]
    scaled = (rates[:, :, None] * values.reshape(length, head_count, -1).astype(jnp.float32)).astype(jnp.bfloat16).astype(jnp.float32)
    step_second = jnp.einsum('thd,htf->hdf', scaled, hidden.astype(jnp.float32))
    back = jnp.einsum('thd,hdf->htf', scaled, weights[2].astype(jnp.float32))
    sig_gate = jax.nn.sigmoid(pre_gate)
    d_gate = (back * pre_up * sig_gate * (1.0 + pre_gate * (1.0 - sig_gate))).astype(jnp.bfloat16).astype(jnp.float32)
    d_up = (back * pre_gate * sig_gate).astype(jnp.bfloat16).astype(jnp.float32)
    step_first = jnp.einsum('htf,thd->hfd', d_gate, shaped)
    step_third = jnp.einsum('htf,thd->hfd', d_up, shaped)
    return (step_first, step_third, step_second)

def step_all(weights, keys, values, rates):
    width = keys.shape[1]
    key_blocks = keys.reshape(CH // TOK_DEV, TOK_DEV, width)
    value_blocks = values.reshape(CH // TOK_DEV, TOK_DEV, width)
    rate_blocks = rates.reshape(CH // TOK_DEV, TOK_DEV, rates.shape[1])
    start = tuple((jnp.zeros(w.shape, jnp.float32) for w in weights))

    def advance(carry, pieces):
        terms = step_block(weights, pieces[0], pieces[1], pieces[2])
        return (tuple((c + s for c, s in zip(carry, terms))), None)
    total, unused = lax.scan(advance, start, (key_blocks, value_blocks, rate_blocks))
    return total

def renorm(old, moved):
    old_norm = jnp.sqrt(lax.optimization_barrier(jnp.sum(old * old, axis=-1, keepdims=True)) + 1e-06)
    moved_norm = jnp.sqrt(lax.optimization_barrier(jnp.sum(moved * moved, axis=-1, keepdims=True)) + 1e-06)
    return moved * old_norm / moved_norm

def reference(query_tokens, key_tokens, value_tokens, learn_rates, fast_first, fast_third, fast_second, momentum_decay):
    start_low = (fast_first, fast_third, fast_second)
    weights0 = tuple((w.astype(jnp.float32) for w in start_low))
    out_zero = apply_all(start_low, query_tokens[0])
    step0 = step_all(start_low, key_tokens[0], value_tokens[0], learn_rates[0])
    step1 = step_all(start_low, key_tokens[1], value_tokens[1], learn_rates[1])
    weights1 = tuple((renorm(w, w + m) for w, m in zip(weights0, step0)))
    low_one = tuple((w.astype(jnp.bfloat16) for w in weights1))
    out_one = apply_all(low_one, query_tokens[1])
    decay = momentum_decay[:, None, None]
    mom2 = tuple((decay * m + s for m, s in zip(step0, step1)))
    weights2 = tuple((renorm(w, w + m) for w, m in zip(weights1, mom2)))
    low_two = tuple((w.astype(jnp.bfloat16) for w in weights2))
    out_two = apply_all(low_two, query_tokens[2])
    return jnp.stack([out_zero, out_one, out_two]).astype(jnp.bfloat16)
```

```python
import functools

import jax
import jax.numpy as jnp
from jax import lax
from jax.experimental import pallas as pl
from jax.experimental.pallas import tpu as pltpu
from jax.sharding import PartitionSpec as P

MESH = pl.DeviceIdType.MESH


def forward_parts(weights, inputs):
    first, third, second = weights
    length = inputs.shape[0]
    head_count = first.shape[0]
    shaped = inputs.reshape(length, head_count, -1)
    pre_gate = jnp.einsum("thd,hfd->htf", shaped, first, preferred_element_type=jnp.float32)
    pre_up = jnp.einsum("thd,hfd->htf", shaped, third, preferred_element_type=jnp.float32)
    hidden = (jax.nn.silu(pre_gate) * pre_up).astype(jnp.bfloat16)
    return (shaped, pre_gate, pre_up, hidden)


def apply_block(weights, inputs):
    shaped, pre_gate, pre_up, hidden = forward_parts(weights, inputs)
    result = jnp.einsum("htf,hdf->thd", hidden, weights[2], preferred_element_type=jnp.float32)
    return result.reshape(inputs.shape[0], -1).astype(jnp.bfloat16)


def partial_steps(weights, keys, values, rates):
    shaped, pre_gate, pre_up, hidden = forward_parts(weights, keys)
    length = keys.shape[0]
    head_count = weights[0].shape[0]
    scaled = (
        rates[:, :, None] * values.reshape(length, head_count, -1).astype(jnp.float32)
    ).astype(jnp.bfloat16)
    step_second = jnp.einsum("thd,htf->hdf", scaled, hidden, preferred_element_type=jnp.float32)
    back = jnp.einsum("thd,hdf->htf", scaled, weights[2], preferred_element_type=jnp.float32)
    sig_gate = jax.nn.sigmoid(pre_gate)
    d_gate = (back * pre_up * sig_gate * (1.0 + pre_gate * (1.0 - sig_gate))).astype(jnp.bfloat16)
    d_up = (back * pre_gate * sig_gate).astype(jnp.bfloat16)
    step_first = jnp.einsum("htf,thd->hfd", d_gate, shaped, preferred_element_type=jnp.float32)
    step_third = jnp.einsum("htf,thd->hfd", d_up, shaped, preferred_element_type=jnp.float32)
    return (step_first, step_third, step_second)


def renorm(old, moved):
    old_norm = jnp.sqrt(jnp.sum(old * old, axis=-1, keepdims=True) + 1e-06)
    moved_norm = jnp.sqrt(jnp.sum(moved * moved, axis=-1, keepdims=True) + 1e-06)
    return moved * old_norm / moved_norm


def shards(
    query_tokens,
    key_tokens,
    value_tokens,
    learn_rates,
    fast_first,
    fast_third,
    fast_second,
    momentum_decay,
):
    owned_zero = jnp.stack([fast_first, fast_third, fast_second])
    full_zero = lax.all_gather(owned_zero, "tok", axis=2, tiled=True)
    terms_zero = partial_steps(full_zero, key_tokens[0], value_tokens[0], learn_rates[0])
    terms_one = partial_steps(full_zero, key_tokens[1], value_tokens[1], learn_rates[1])
    step_zero = lax.psum_scatter(
        jnp.stack(terms_zero).astype(jnp.bfloat16), "tok", scatter_dimension=2, tiled=True
    ).astype(jnp.float32)
    step_one = lax.psum_scatter(
        jnp.stack(terms_one).astype(jnp.bfloat16), "tok", scatter_dimension=2, tiled=True
    ).astype(jnp.float32)
    out_zero = apply_block(full_zero, query_tokens[0])
    decay = momentum_decay[None, :, None, None]
    weights_zero = owned_zero.astype(jnp.float32)
    weights_one = renorm(weights_zero, weights_zero + step_zero)
    full_one = lax.all_gather(weights_one.astype(jnp.bfloat16), "tok", axis=2, tiled=True)
    weights_two = renorm(weights_one, weights_one + decay * step_zero + step_one)
    full_two = lax.all_gather(weights_two.astype(jnp.bfloat16), "tok", axis=2, tiled=True)
    out_one = apply_block(full_one, query_tokens[1])
    out_two = apply_block(full_two, query_tokens[2])
    return jnp.stack([out_zero, out_one, out_two])


def dot_nt(a, b):
    return lax.dot_general(a, b, (((1,), (1,)), ((), ())), preferred_element_type=jnp.float32)


def dot_nn(a, b):
    return lax.dot_general(a, b, (((1,), (0,)), ((), ())), preferred_element_type=jnp.float32)


def dot_tn(a, b):
    return lax.dot_general(a, b, (((0,), (0,)), ((), ())), preferred_element_type=jnp.float32)


def kernel(
    chips,
    query_ref,
    key_ref,
    value_ref,
    rate_ref,
    first_ref,
    third_ref,
    second_ref,
    decay_ref,
    out_ref,
    queries,
    keys,
    values,
    rates,
    full,
    part,
    stage,
    landed,
    step_own,
    weight_own,
    result,
    gates,
    ups,
    hiddens,
    swap_send,
    swap_recv,
    local_sem,
    gather_send,
    gather_recv,
    sum_send,
    sum_recv,
    out_send,
    out_recv,
    out_local,
):
    index = lax.axis_index("tok")
    chip = index // 2
    core = index % 2
    odd = chip % 2
    place = (1 - odd) * (chip // 2) + odd * (chips - 1 - chip // 2)
    half = chips // 2

    def chip_at(position):
        wrapped = (position + chips) % chips
        back = wrapped // half
        return (1 - back) * (2 * wrapped) + back * (2 * (chips - 1 - wrapped) + 1)

    partner = {"tok": index + 1 - 2 * core}
    sides = (
        {"tok": 2 * chip_at(place + 1) + core},
        {"tok": 2 * chip_at(place - 1) + core},
    )
    rows = first_ref.shape[1]
    block = 2 * rows
    tokens = key_ref.shape[1]
    width = first_ref.shape[2]
    cut = width // 2

    barrier = pltpu.get_barrier_semaphore()
    for other in (partner,) + sides:
        pl.semaphore_signal(barrier, inc=1, device_id=other, device_id_type=MESH)
    pl.semaphore_wait(barrier, 3)

    mine = pl.ds(pl.multiple_of(core * width, width), width)
    theirs = pl.ds(pl.multiple_of((1 - core) * width, width), width)
    slot = pl.ds(pl.multiple_of(core * tokens, tokens), tokens)
    other_slot = pl.ds(pl.multiple_of((1 - core) * tokens, tokens), tokens)
    shard = pl.ds(pl.multiple_of(index * rows, rows), rows)

    pairs = []
    for m, ref in enumerate((first_ref, third_ref, second_ref)):
        pairs.append((ref.at[1 - core], ref.at[core], full.at[0, m, shard, :]))
    for b in range(2):
        pairs.append((key_ref.at[b, :, theirs], key_ref.at[b, :, mine], keys.at[b, slot, :]))
        pairs.append((value_ref.at[b, :, theirs], value_ref.at[b, :, mine], values.at[b, slot, :]))
        pairs.append((rate_ref.at[b], rate_ref.at[b], rates.at[b, slot, :]))
    for b in range(3):
        pairs.append((query_ref.at[b, :, theirs], query_ref.at[b, :, mine], queries.at[b, slot, :]))
    swaps = []
    locals_ = []
    for n, (away, here, target) in enumerate(pairs):
        swap = pltpu.make_async_remote_copy(
            src_ref=away,
            dst_ref=target,
            send_sem=swap_send.at[n],
            recv_sem=swap_recv.at[n],
            device_id=partner,
            device_id_type=MESH,
        )
        swap.start()
        kept = pltpu.make_async_copy(here, target, local_sem.at[n])
        kept.start()
        swaps.append(swap)
        locals_.append(kept)

    def ready(n):
        swaps[n].wait_recv()
        locals_[n].wait()

    def rows_of(owner):
        return pl.ds(pl.multiple_of(owner * block, block), block)

    def cols_of(way):
        return pl.ds(way * cut, cut)

    sent = []

    def gather_copy(k, m, way, s):
        owner = chip_at(place - (s - 1)) if way == 0 else chip_at(place + (s - 1))
        span = full.at[k, m, rows_of(owner), cols_of(way) if s == half else pl.ds(0, width)]
        return pltpu.make_async_remote_copy(
            src_ref=span,
            dst_ref=span,
            send_sem=gather_send.at[k, m, way, s - 1],
            recv_sem=gather_recv.at[k, m, way, s - 1],
            device_id=sides[way],
            device_id_type=MESH,
        )

    def gather_start(k, m, way, s):
        copy = gather_copy(k, m, way, s)
        copy.start()
        sent.append(copy)

    def gather_step(k, s, order=(0, 1, 2)):
        for m in order:
            for way in range(2):
                gather_copy(k, m, way, s).wait_recv()
                if s < half:
                    gather_start(k, m, way, s + 1)

    def sum_copy(t, way, s):
        span = cols_of(way) if s == 1 else pl.ds(0, width)
        return pltpu.make_async_remote_copy(
            src_ref=stage.at[t, way, s - 1, :, span],
            dst_ref=landed.at[t, way, s - 1, :, span],
            send_sem=sum_send.at[t, way, s - 1],
            recv_sem=sum_recv.at[t, way, s - 1],
            device_id=sides[way],
            device_id_type=MESH,
        )

    def sum_start(t, way, s):
        ahead = half - s + 1
        owner = chip_at(place + ahead) if way == 0 else chip_at(place - ahead)
        span = cols_of(way)
        if s == 1:
            stage[t, way, 0, :, span] = part[t, rows_of(owner), span].astype(jnp.bfloat16)
        elif s == 2:
            rest = cols_of(1 - way)
            stage[t, way, 1, :, span] = (
                part[t, rows_of(owner), span] + landed[t, way, 0, :, span].astype(jnp.float32)
            ).astype(jnp.bfloat16)
            stage[t, way, 1, :, rest] = part[t, rows_of(owner), rest].astype(jnp.bfloat16)
        else:
            stage[t, way, s - 1] = (
                part[t, rows_of(owner), :] + landed[t, way, s - 2].astype(jnp.float32)
            ).astype(jnp.bfloat16)
        copy = sum_copy(t, way, s)
        copy.start()
        sent.append(copy)

    order = (2, 0, 1)

    def sum_step(j, s):
        for m in order:
            for way in range(2):
                sum_copy(3 * j + m, way, s).wait_recv()
                sum_start(3 * j + m, way, s + 1)

    def total_of(t):
        for way in range(2):
            sum_copy(t, way, half).wait_recv()
        own = part[t, rows_of(chip), :]
        return (
            own
            + landed[t, 0, half - 1].astype(jnp.float32)
            + landed[t, 1, half - 1].astype(jnp.float32)
        )

    def forward(k, x):
        gate = dot_nt(x, full[k, 0])
        up = dot_nt(x, full[k, 1])
        sig = jax.nn.sigmoid(gate)
        return gate, up, sig, (gate * sig * up).astype(jnp.bfloat16)

    def keys_forward(j):
        gate, up, sig, hidden = forward(0, keys[j])
        gates[...] = gate
        ups[...] = up
        hiddens[...] = hidden

    def steps(j):
        rate = jnp.where(core == 0, rates[j, :, 0:1], rates[j, :, 1:2])
        scaled = (rate * values[j].astype(jnp.float32)).astype(jnp.bfloat16)
        part[3 * j + 2] = dot_tn(scaled, hiddens[...])
        for way in range(2):
            sum_start(3 * j + 2, way, 1)
        back = dot_nn(scaled, full[0, 2])
        gate = gates[...]
        sig = jax.nn.sigmoid(gate)
        x = keys[j]
        d_gate = (back * ups[...] * sig * (1.0 + gate * (1.0 - sig))).astype(jnp.bfloat16)
        part[3 * j] = dot_tn(d_gate, x)
        for way in range(2):
            sum_start(3 * j, way, 1)
        d_up = (back * gate * sig).astype(jnp.bfloat16)
        part[3 * j + 1] = dot_tn(d_up, x)
        for way in range(2):
            sum_start(3 * j + 1, way, 1)

    outs = []

    def read_hidden(k):
        gate, up, sig, hidden = forward(k, queries[k])
        hiddens[...] = hidden

    def read_out(k):
        result[k] = dot_nt(hiddens[...], full[k, 2]).astype(jnp.bfloat16)
        away = pltpu.make_async_remote_copy(
            src_ref=result.at[k, other_slot, :],
            dst_ref=out_ref.at[k, :, mine],
            send_sem=out_send.at[k],
            recv_sem=out_recv.at[k],
            device_id=partner,
            device_id_type=MESH,
        )
        away.start()
        here = pltpu.make_async_copy(
            result.at[k, slot, :], out_ref.at[k, :, mine], out_local.at[k]
        )
        here.start()
        outs.append((away, here))

    for m in range(3):
        ready(m)
        for way in range(2):
            gather_start(0, m, way, 1)
    for s in range(1, half + 1):
        gather_step(0, s)

    for n in range(3, len(pairs)):
        ready(n)
    keys_forward(0)
    steps(0)
    keys_forward(1)
    sum_step(0, 1)
    steps(1)
    later = [functools.partial(read_hidden, 0), functools.partial(read_out, 0)]
    for s in range(2, half):
        sum_step(0, s)
        sum_step(1, s - 1)
        if s == 2:
            for piece in later:
                piece()
    decay = decay_ref[core]
    for m in order:
        moment = total_of(m)
        step_own[m] = moment
        old = full[0, m, rows_of(chip), :].astype(jnp.float32)
        fresh = renorm(old, old + moment)
        weight_own[m] = fresh
        full[1, m, rows_of(chip), :] = fresh.astype(jnp.bfloat16)
        for way in range(2):
            gather_start(1, m, way, 1)
    sum_step(1, half - 1)
    gather_step(1, 1, order)
    for m in order:
        moment = decay * step_own[m] + total_of(3 + m)
        old = weight_own[m]
        fresh = renorm(old, old + moment)
        full[2, m, rows_of(chip), :] = fresh.astype(jnp.bfloat16)
        for way in range(2):
            gather_start(2, m, way, 1)
    for s in range(2, half + 1):
        gather_step(1, s, order)
        if s < half:
            gather_step(2, s - 1, (0, 1, 2))
    read_hidden(1)
    read_out(1)
    gather_step(2, half - 1, (0, 1, 2))
    gather_step(2, half, (0, 1))
    read_hidden(2)
    gather_step(2, half, (2,))
    read_out(2)

    for n in range(len(pairs)):
        swaps[n].wait_send()
    for copy in sent:
        copy.wait_send()
    for away, here in outs:
        here.wait()
        away.wait()


def fused_shards(chips, query, key, value, rate, first, third, second, decay):
    blocks, tokens, features = query.shape
    heads, rows, width = first.shape
    half = chips // 2
    hidden = 2 * rows * chips
    span = 2 * tokens
    anywhere = pl.BlockSpec(memory_space=pl.ANY)
    dma = pltpu.SemaphoreType.DMA
    low, wide = jnp.bfloat16, jnp.float32
    return pl.pallas_call(
        functools.partial(kernel, chips),
        out_shape=jax.ShapeDtypeStruct(query.shape, low),
        in_specs=[anywhere] * 7 + [pl.BlockSpec(memory_space=pltpu.SMEM)],
        out_specs=anywhere,
        scratch_shapes=[
            pltpu.VMEM((3, span, width), low),
            pltpu.VMEM((2, span, width), low),
            pltpu.VMEM((2, span, width), low),
            pltpu.VMEM((2, span, heads), wide),
            pltpu.VMEM((3, 3, hidden, width), low),
            pltpu.VMEM((6, hidden, width), wide),
            pltpu.VMEM((6, 2, half, 2 * rows, width), low),
            pltpu.VMEM((6, 2, half, 2 * rows, width), low),
            pltpu.VMEM((3, 2 * rows, width), wide),
            pltpu.VMEM((3, 2 * rows, width), wide),
            pltpu.VMEM((3, span, width), low),
            pltpu.VMEM((span, hidden), wide),
            pltpu.VMEM((span, hidden), wide),
            pltpu.VMEM((span, hidden), low),
            dma((12,)),
            dma((12,)),
            dma((12,)),
            dma((3, 3, 2, half)),
            dma((3, 3, 2, half)),
            dma((6, 2, half)),
            dma((6, 2, half)),
            dma((3,)),
            dma((3,)),
            dma((3,)),
        ],
        compiler_params=pltpu.CompilerParams(
            collective_id=0, has_side_effects=True, vmem_limit_bytes=60 * 1024 * 1024
        ),
    )(query, key, value, rate, first, third, second, decay)


def solution(mesh):
    placed = (
        P(None, ("groups", "tok"), None),
        P(None, ("groups", "tok"), None),
        P(None, ("groups", "tok"), None),
        P(None, ("groups", "tok"), None),
        P(None, "tok", None),
        P(None, "tok", None),
        P(None, "tok", None),
        P(),
    )
    chips = mesh.shape["tok"] // 2

    def body(*arrays):
        rows = arrays[4].shape[1]
        if rows % 16 or chips % 2 or chips < 4:
            return shards(*arrays)
        return fused_shards(chips, *arrays)

    return jax.shard_map(
        body,
        mesh=mesh,
        in_specs=placed,
        out_specs=P(None, ("groups", "tok"), None),
        check_vma=False,
    )
```

```python
import jax
import jax.numpy as jnp
from jax import lax
from jax.experimental import pallas as pl
from jax.experimental.pallas import tpu as pltpu
from jax.sharding import PartitionSpec as P

MESH = pl.DeviceIdType.MESH


def forward_parts(weights, inputs):
    first, third, second = weights
    length = inputs.shape[0]
    head_count = first.shape[0]
    shaped = inputs.reshape(length, head_count, -1)
    pre_gate = jnp.einsum("thd,hfd->htf", shaped, first, preferred_element_type=jnp.float32)
    pre_up = jnp.einsum("thd,hfd->htf", shaped, third, preferred_element_type=jnp.float32)
    hidden = (jax.nn.silu(pre_gate) * pre_up).astype(jnp.bfloat16)
    return (shaped, pre_gate, pre_up, hidden)


def apply_block(weights, inputs):
    shaped, pre_gate, pre_up, hidden = forward_parts(weights, inputs)
    result = jnp.einsum("htf,hdf->thd", hidden, weights[2], preferred_element_type=jnp.float32)
    return result.reshape(inputs.shape[0], -1).astype(jnp.bfloat16)


def partial_steps(weights, keys, values, rates):
    shaped, pre_gate, pre_up, hidden = forward_parts(weights, keys)
    length = keys.shape[0]
    head_count = weights[0].shape[0]
    scaled = (
        rates[:, :, None] * values.reshape(length, head_count, -1).astype(jnp.float32)
    ).astype(jnp.bfloat16)
    step_second = jnp.einsum("thd,htf->hdf", scaled, hidden, preferred_element_type=jnp.float32)
    back = jnp.einsum("thd,hdf->htf", scaled, weights[2], preferred_element_type=jnp.float32)
    sig_gate = jax.nn.sigmoid(pre_gate)
    d_gate = (back * pre_up * sig_gate * (1.0 + pre_gate * (1.0 - sig_gate))).astype(jnp.bfloat16)
    d_up = (back * pre_gate * sig_gate).astype(jnp.bfloat16)
    step_first = jnp.einsum("htf,thd->hfd", d_gate, shaped, preferred_element_type=jnp.float32)
    step_third = jnp.einsum("htf,thd->hfd", d_up, shaped, preferred_element_type=jnp.float32)
    return (step_first, step_third, step_second)


def renorm(old, moved):
    old_norm = jnp.sqrt(jnp.sum(old * old, axis=-1, keepdims=True) + 1e-06)
    moved_norm = jnp.sqrt(jnp.sum(moved * moved, axis=-1, keepdims=True) + 1e-06)
    return moved * old_norm / moved_norm


def shards(
    query_tokens,
    key_tokens,
    value_tokens,
    learn_rates,
    fast_first,
    fast_third,
    fast_second,
    momentum_decay,
):
    owned_zero = jnp.stack([fast_first, fast_third, fast_second])
    full_zero = lax.all_gather(owned_zero, "tok", axis=2, tiled=True)
    terms_zero = partial_steps(full_zero, key_tokens[0], value_tokens[0], learn_rates[0])
    terms_one = partial_steps(full_zero, key_tokens[1], value_tokens[1], learn_rates[1])
    step_zero = lax.psum_scatter(
        jnp.stack(terms_zero).astype(jnp.bfloat16), "tok", scatter_dimension=2, tiled=True
    ).astype(jnp.float32)
    step_one = lax.psum_scatter(
        jnp.stack(terms_one).astype(jnp.bfloat16), "tok", scatter_dimension=2, tiled=True
    ).astype(jnp.float32)
    out_zero = apply_block(full_zero, query_tokens[0])
    decay = momentum_decay[None, :, None, None]
    weights_zero = owned_zero.astype(jnp.float32)
    weights_one = renorm(weights_zero, weights_zero + step_zero)
    full_one = lax.all_gather(weights_one.astype(jnp.bfloat16), "tok", axis=2, tiled=True)
    weights_two = renorm(weights_one, weights_one + decay * step_zero + step_one)
    full_two = lax.all_gather(weights_two.astype(jnp.bfloat16), "tok", axis=2, tiled=True)
    out_one = apply_block(full_one, query_tokens[1])
    out_two = apply_block(full_two, query_tokens[2])
    return jnp.stack([out_zero, out_one, out_two])


def dot_nt(a, b):
    return lax.dot_general(a, b, (((1,), (1,)), ((), ())), preferred_element_type=jnp.float32)


def dot_nn(a, b):
    return lax.dot_general(a, b, (((1,), (0,)), ((), ())), preferred_element_type=jnp.float32)


def dot_tn(a, b):
    return lax.dot_general(a, b, (((0,), (0,)), ((), ())), preferred_element_type=jnp.float32)


def kernel(
    query_ref,
    key_ref,
    value_ref,
    rate_ref,
    first_ref,
    third_ref,
    second_ref,
    decay_ref,
    out_ref,
    queries,
    keys,
    values,
    rates,
    full,
    part,
    core_out,
    core_in,
    side_out,
    side_in,
    far_out,
    far_in,
    step_own,
    weight_own,
    result,
    gates,
    ups,
    hiddens,
    swap_send,
    swap_recv,
    local_sem,
    gather_send,
    gather_recv,
    sum_send,
    sum_recv,
    out_send,
    out_recv,
    out_local,
):
    index = lax.axis_index("tok")
    core = index % 2
    lane = (index // 2) % 2
    head = (index // 4) % 2
    pair = index // 8
    partner = {"tok": index + 1 - 2 * core}
    beside = {"tok": index + 2 - 4 * lane}
    mate = {"tok": index + 4 - 8 * head}
    beyond = {"tok": index + 8 - 16 * pair}
    rows = first_ref.shape[1]
    tokens = key_ref.shape[1]
    width = first_ref.shape[2]
    hidden_units = 16 * rows

    barrier = pltpu.get_barrier_semaphore()
    for other in (partner, beside, mate, beyond):
        pl.semaphore_signal(barrier, inc=1, device_id=other, device_id_type=MESH)
    pl.semaphore_wait(barrier, 4)

    sent = []

    def push(src, dst, send_sem, recv_sem, to):
        return pltpu.make_async_remote_copy(
            src_ref=src,
            dst_ref=dst,
            send_sem=send_sem,
            recv_sem=recv_sem,
            device_id=to,
            device_id_type=MESH,
        )

    def go(copy):
        copy.start()
        sent.append(copy)

    mine = pl.ds(pl.multiple_of(head * width, width), width)
    theirs = pl.ds(pl.multiple_of((1 - head) * width, width), width)
    slot = pl.ds(pl.multiple_of(head * tokens, tokens), tokens)
    other_slot = pl.ds(pl.multiple_of((1 - head) * tokens, tokens), tokens)

    pairs = []
    for m, ref in enumerate((first_ref, third_ref, second_ref)):
        pairs.append((ref.at[1 - head], ref.at[head], full.at[0, m, pair, head, lane, core]))
    for b in range(2):
        pairs.append((key_ref.at[b, :, theirs], key_ref.at[b, :, mine], keys.at[b, slot, :]))
        pairs.append((value_ref.at[b, :, theirs], value_ref.at[b, :, mine], values.at[b, slot, :]))
        pairs.append((rate_ref.at[b], rate_ref.at[b], rates.at[b, :, slot]))
    for b in range(3):
        pairs.append((query_ref.at[b, :, theirs], query_ref.at[b, :, mine], queries.at[b, slot, :]))
    swaps = {}
    locals_ = {}

    def swap(first, last):
        for n in range(first, last):
            away, here, target = pairs[n]
            swaps[n] = push(away, target, swap_send.at[n], swap_recv.at[n], mate)
            swaps[n].start()
            locals_[n] = pltpu.make_async_copy(here, target, local_sem.at[n])
            locals_[n].start()

    def ready(n):
        swaps[n].wait_recv()
        locals_[n].wait()

    def block_of(k, m, p, q):
        return full.at[k, m, p, :, q, core]

    def gather_copy(k, m, n):
        p, q = (
            (pair, lane),
            (pair, lane),
            (1 - pair, lane),
            (pair, lane),
            (1 - pair, lane),
            (pair, 1 - lane),
            (1 - pair, 1 - lane),
        )[n]
        span = block_of(k, m, p, q)
        to = (beyond, beside, beside, partner, partner, partner, partner)[n]
        return push(span, span, gather_send.at[k, m, n], gather_recv.at[k, m, n], to)

    def gather_own(k, m):
        for n in (0, 1, 3):
            go(gather_copy(k, m, n))

    def gather_beyond(k, m):
        gather_copy(k, m, 0).wait_recv()
        go(gather_copy(k, m, 2))
        go(gather_copy(k, m, 4))

    def gather_beside(k, m, n):
        gather_copy(k, m, n).wait_recv()
        go(gather_copy(k, m, n + 4))

    def gather_end(k, m):
        for n in range(3, 7):
            gather_copy(k, m, n).wait_recv()

    def core_copy(t):
        return push(
            core_out.at[t], core_in.at[t], sum_send.at[t, 0], sum_recv.at[t, 0], partner
        )

    def side_copy(t, p, n):
        return push(
            side_out.at[t, p], side_in.at[t, p], sum_send.at[t, n], sum_recv.at[t, n], beside
        )

    def far_copy(t):
        return push(far_out.at[t], far_in.at[t], sum_send.at[t, 3], sum_recv.at[t, 3], beyond)

    def core_start(t):
        core_out[t] = part[t, :, :, :, 1 - core].astype(jnp.bfloat16)
        go(core_copy(t))

    def core_sum(t, p, q):
        return part[t, p, :, q, core] + core_in[t, p, :, q].astype(jnp.float32)

    def side_start(t):
        core_copy(t).wait_recv()
        for n, p in ((1, 1 - pair), (2, pair)):
            side_out[t, p] = core_sum(t, p, 1 - lane).astype(jnp.bfloat16)
            go(side_copy(t, p, n))

    def far_start(t):
        p = 1 - pair
        side_copy(t, p, 1).wait_recv()
        far_out[t] = (core_sum(t, p, lane) + side_in[t, p].astype(jnp.float32)).astype(
            jnp.bfloat16
        )
        go(far_copy(t))

    def total_of(t):
        side_copy(t, pair, 2).wait_recv()
        near = core_sum(t, pair, lane) + side_in[t, pair].astype(jnp.float32)
        far_copy(t).wait_recv()
        return near + far_in[t].astype(jnp.float32)

    order = (2, 0, 1)

    def whole(k, m):
        return full[k, m].reshape(hidden_units, width)

    def forward(k, x):
        gate = dot_nt(x, whole(k, 0))
        up = dot_nt(x, whole(k, 1))
        sig = jax.nn.sigmoid(gate)
        return gate, up, sig, (gate * sig * up).astype(jnp.bfloat16)

    def keys_forward(j):
        gate, up, sig, hidden = forward(0, keys[j])
        gates[...] = gate
        ups[...] = up
        hiddens[...] = hidden

    def steps(j):
        row = jnp.where(head == 0, rates[j, 0:1, :], rates[j, 1:2, :])
        rate = jnp.transpose(jnp.broadcast_to(row, (128, row.shape[1])))[:, 0:1]
        scaled = (rate * values[j].astype(jnp.float32)).astype(jnp.bfloat16)
        part[3 * j + 2] = dot_tn(scaled, hiddens[...]).reshape(part.shape[1:])
        core_start(3 * j + 2)
        back = dot_nn(scaled, whole(0, 2))
        gate = gates[...]
        sig = jax.nn.sigmoid(gate)
        x = keys[j]
        d_gate = (back * ups[...] * sig * (1.0 + gate * (1.0 - sig))).astype(jnp.bfloat16)
        part[3 * j] = dot_tn(d_gate, x).reshape(part.shape[1:])
        core_start(3 * j)
        d_up = (back * gate * sig).astype(jnp.bfloat16)
        part[3 * j + 1] = dot_tn(d_up, x).reshape(part.shape[1:])
        core_start(3 * j + 1)

    outs = []

    def read_hidden(k):
        gate, up, sig, hidden = forward(k, queries[k])
        hiddens[...] = hidden

    def read_out(k):
        result[k] = dot_nt(hiddens[...], whole(k, 2)).astype(jnp.bfloat16)
        away = push(
            result.at[k, other_slot, :],
            out_ref.at[k, :, mine],
            out_send.at[k],
            out_recv.at[k],
            mate,
        )
        away.start()
        here = pltpu.make_async_copy(
            result.at[k, slot, :], out_ref.at[k, :, mine], out_local.at[k]
        )
        here.start()
        outs.append((away, here))

    swap(0, 6)
    for m in range(3):
        ready(m)
        gather_own(0, m)
    swap(6, 9)
    for m in range(3):
        gather_beyond(0, m)
        gather_beside(0, m, 1)
    for m in range(3):
        gather_beside(0, m, 2)
    for m in range(3):
        gather_end(0, m)
    for n in range(3, 6):
        ready(n)
    keys_forward(0)
    steps(0)
    for m in order:
        side_start(m)
    swap(9, 11)
    for n in range(6, 9):
        ready(n)
    keys_forward(1)
    steps(1)
    for m in order:
        far_start(m)
        side_start(3 + m)
    ready(9)
    read_hidden(0)
    read_out(0)
    swap(11, 12)
    for m in order:
        moment = total_of(m)
        step_own[m] = moment
        old = full[0, m, pair, :, lane, core].astype(jnp.float32)
        fresh = renorm(old, old + moment)
        weight_own[m] = fresh
        full[1, m, pair, :, lane, core] = fresh.astype(jnp.bfloat16)
        gather_own(1, m)
    decay = decay_ref[head]
    for m in order:
        far_start(3 + m)
    for m in order:
        gather_beyond(1, m)
        gather_beside(1, m, 1)
    for m in order:
        moment = decay * step_own[m] + total_of(3 + m)
        old = weight_own[m]
        fresh = renorm(old, old + moment)
        full[2, m, pair, :, lane, core] = fresh.astype(jnp.bfloat16)
        gather_own(2, m)
    for m in order:
        gather_beside(1, m, 2)
    for m in order:
        gather_beyond(2, m)
        gather_beside(2, m, 1)
    for m in range(3):
        gather_end(1, m)
    ready(10)
    ready(11)
    read_hidden(1)
    read_out(1)
    for m in order:
        gather_beside(2, m, 2)
    for m in (0, 1):
        gather_end(2, m)
    read_hidden(2)
    gather_end(2, 2)
    read_out(2)

    for n in range(len(pairs)):
        swaps[n].wait_send()
    for copy in sent:
        copy.wait_send()
    for away, here in outs:
        here.wait()
        away.wait()


def fused_shards(query, key, value, rate, first, third, second, decay):
    blocks, tokens, features = query.shape
    heads, rows, width = first.shape
    hidden = 16 * rows
    span = 2 * tokens
    anywhere = pl.BlockSpec(memory_space=pl.ANY)
    dma = pltpu.SemaphoreType.DMA
    low, wide = jnp.bfloat16, jnp.float32
    return pl.pallas_call(
        kernel,
        out_shape=jax.ShapeDtypeStruct(query.shape, low),
        in_specs=[anywhere] * 7 + [pl.BlockSpec(memory_space=pltpu.SMEM)],
        out_specs=anywhere,
        scratch_shapes=[
            pltpu.VMEM((3, span, width), low),
            pltpu.VMEM((2, span, width), low),
            pltpu.VMEM((2, span, width), low),
            pltpu.VMEM((2, heads, span), wide),
            pltpu.VMEM((3, 3, 2, 2, 2, 2, rows, width), low),
            pltpu.VMEM((6, 2, 2, 2, 2, rows, width), wide),
            pltpu.VMEM((6, 2, 2, 2, rows, width), low),
            pltpu.VMEM((6, 2, 2, 2, rows, width), low),
            pltpu.VMEM((6, 2, 2, rows, width), low),
            pltpu.VMEM((6, 2, 2, rows, width), low),
            pltpu.VMEM((6, 2, rows, width), low),
            pltpu.VMEM((6, 2, rows, width), low),
            pltpu.VMEM((3, 2, rows, width), wide),
            pltpu.VMEM((3, 2, rows, width), wide),
            pltpu.VMEM((3, span, width), low),
            pltpu.VMEM((span, hidden), wide),
            pltpu.VMEM((span, hidden), wide),
            pltpu.VMEM((span, hidden), low),
            dma((12,)),
            dma((12,)),
            dma((12,)),
            dma((3, 3, 7)),
            dma((3, 3, 7)),
            dma((6, 4)),
            dma((6, 4)),
            dma((3,)),
            dma((3,)),
            dma((3,)),
        ],
        compiler_params=pltpu.CompilerParams(
            collective_id=0, has_side_effects=True, vmem_limit_bytes=60 * 1024 * 1024
        ),
    )(query, key, value, jnp.swapaxes(rate, 1, 2), first, third, second, decay)


def solution(mesh):
    placed = (
        P(None, ("groups", "tok"), None),
        P(None, ("groups", "tok"), None),
        P(None, ("groups", "tok"), None),
        P(None, ("groups", "tok"), None),
        P(None, "tok", None),
        P(None, "tok", None),
        P(None, "tok", None),
        P(),
    )
    chips = mesh.shape["tok"] // 2

    def body(*arrays):
        rows = arrays[4].shape[1]
        if rows % 16 or chips != 8 or arrays[4].shape[0] != 2:
            return shards(*arrays)
        return fused_shards(*arrays)

    return jax.shard_map(
        body,
        mesh=mesh,
        in_specs=placed,
        out_specs=P(None, ("groups", "tok"), None),
        check_vma=False,
    )
```

```python
import jax
import jax.numpy as jnp
from jax import lax
from jax.experimental import pallas as pl
from jax.experimental.pallas import tpu as pltpu
from jax.sharding import PartitionSpec as P

MESH = pl.DeviceIdType.MESH


def forward_parts(weights, inputs):
    first, third, second = weights
    length = inputs.shape[0]
    head_count = first.shape[0]
    shaped = inputs.reshape(length, head_count, -1)
    pre_gate = jnp.einsum("thd,hfd->htf", shaped, first, preferred_element_type=jnp.float32)
    pre_up = jnp.einsum("thd,hfd->htf", shaped, third, preferred_element_type=jnp.float32)
    hidden = (jax.nn.silu(pre_gate) * pre_up).astype(jnp.bfloat16)
    return (shaped, pre_gate, pre_up, hidden)


def apply_block(weights, inputs):
    shaped, pre_gate, pre_up, hidden = forward_parts(weights, inputs)
    result = jnp.einsum("htf,hdf->thd", hidden, weights[2], preferred_element_type=jnp.float32)
    return result.reshape(inputs.shape[0], -1).astype(jnp.bfloat16)


def partial_steps(weights, keys, values, rates):
    shaped, pre_gate, pre_up, hidden = forward_parts(weights, keys)
    length = keys.shape[0]
    head_count = weights[0].shape[0]
    scaled = (
        rates[:, :, None] * values.reshape(length, head_count, -1).astype(jnp.float32)
    ).astype(jnp.bfloat16)
    step_second = jnp.einsum("thd,htf->hdf", scaled, hidden, preferred_element_type=jnp.float32)
    back = jnp.einsum("thd,hdf->htf", scaled, weights[2], preferred_element_type=jnp.float32)
    sig_gate = jax.nn.sigmoid(pre_gate)
    d_gate = (back * pre_up * sig_gate * (1.0 + pre_gate * (1.0 - sig_gate))).astype(jnp.bfloat16)
    d_up = (back * pre_gate * sig_gate).astype(jnp.bfloat16)
    step_first = jnp.einsum("htf,thd->hfd", d_gate, shaped, preferred_element_type=jnp.float32)
    step_third = jnp.einsum("htf,thd->hfd", d_up, shaped, preferred_element_type=jnp.float32)
    return (step_first, step_third, step_second)


def renorm(old, moved):
    old_norm = jnp.sqrt(jnp.sum(old * old, axis=-1, keepdims=True) + 1e-06)
    moved_norm = jnp.sqrt(jnp.sum(moved * moved, axis=-1, keepdims=True) + 1e-06)
    return moved * old_norm / moved_norm


def shards(
    query_tokens,
    key_tokens,
    value_tokens,
    learn_rates,
    fast_first,
    fast_third,
    fast_second,
    momentum_decay,
):
    owned_zero = jnp.stack([fast_first, fast_third, fast_second])
    full_zero = lax.all_gather(owned_zero, "tok", axis=2, tiled=True)
    terms_zero = partial_steps(full_zero, key_tokens[0], value_tokens[0], learn_rates[0])
    terms_one = partial_steps(full_zero, key_tokens[1], value_tokens[1], learn_rates[1])
    step_zero = lax.psum_scatter(
        jnp.stack(terms_zero).astype(jnp.bfloat16), "tok", scatter_dimension=2, tiled=True
    ).astype(jnp.float32)
    step_one = lax.psum_scatter(
        jnp.stack(terms_one).astype(jnp.bfloat16), "tok", scatter_dimension=2, tiled=True
    ).astype(jnp.float32)
    out_zero = apply_block(full_zero, query_tokens[0])
    decay = momentum_decay[None, :, None, None]
    weights_zero = owned_zero.astype(jnp.float32)
    weights_one = renorm(weights_zero, weights_zero + step_zero)
    full_one = lax.all_gather(weights_one.astype(jnp.bfloat16), "tok", axis=2, tiled=True)
    weights_two = renorm(weights_one, weights_one + decay * step_zero + step_one)
    full_two = lax.all_gather(weights_two.astype(jnp.bfloat16), "tok", axis=2, tiled=True)
    out_one = apply_block(full_one, query_tokens[1])
    out_two = apply_block(full_two, query_tokens[2])
    return jnp.stack([out_zero, out_one, out_two])


def dot_nt(a, b):
    return lax.dot_general(a, b, (((1,), (1,)), ((), ())), preferred_element_type=jnp.float32)


def dot_nn(a, b):
    return lax.dot_general(a, b, (((1,), (0,)), ((), ())), preferred_element_type=jnp.float32)


def dot_tn(a, b):
    return lax.dot_general(a, b, (((0,), (0,)), ((), ())), preferred_element_type=jnp.float32)


def kernel(
    query_ref,
    key_ref,
    value_ref,
    rate_ref,
    first_ref,
    third_ref,
    second_ref,
    decay_ref,
    out_ref,
    queries,
    keys,
    values,
    rates,
    full,
    part,
    core_out,
    core_in,
    side_out,
    side_in,
    far_out,
    far_in,
    step_own,
    weight_own,
    result,
    gates,
    ups,
    hiddens,
    swap_send,
    swap_recv,
    local_sem,
    gather_send,
    gather_recv,
    sum_send,
    sum_recv,
    out_send,
    out_recv,
    out_local,
):
    index = lax.axis_index("tok")
    core = index % 2
    lane = (index // 2) % 2
    head = (index // 4) % 2
    pair = index // 8
    partner = {"tok": index + 1 - 2 * core}
    beside = {"tok": index + 2 - 4 * lane}
    mate = {"tok": index + 4 - 8 * head}
    beyond = {"tok": index + 8 - 16 * pair}
    rows = first_ref.shape[1]
    tokens = key_ref.shape[1]
    width = first_ref.shape[2]
    hidden_units = 16 * rows

    barrier = pltpu.get_barrier_semaphore()
    for other in (partner, beside, mate, beyond):
        pl.semaphore_signal(barrier, inc=1, device_id=other, device_id_type=MESH)
    pl.semaphore_wait(barrier, 4)

    sent = []

    def push(src, dst, send_sem, recv_sem, to):
        return pltpu.make_async_remote_copy(
            src_ref=src,
            dst_ref=dst,
            send_sem=send_sem,
            recv_sem=recv_sem,
            device_id=to,
            device_id_type=MESH,
        )

    def go(copy):
        copy.start()
        sent.append(copy)

    mine = pl.ds(pl.multiple_of(head * width, width), width)
    theirs = pl.ds(pl.multiple_of((1 - head) * width, width), width)
    slot = pl.ds(pl.multiple_of(head * tokens, tokens), tokens)
    other_slot = pl.ds(pl.multiple_of((1 - head) * tokens, tokens), tokens)

    pairs = []
    for m, ref in enumerate((first_ref, third_ref, second_ref)):
        pairs.append((ref.at[1 - head], ref.at[head], full.at[0, m, pair, head, lane, core]))
    for b in range(2):
        pairs.append((key_ref.at[b, :, theirs], key_ref.at[b, :, mine], keys.at[b, slot, :]))
        pairs.append((value_ref.at[b, :, theirs], value_ref.at[b, :, mine], values.at[b, slot, :]))
        pairs.append((rate_ref.at[b], rate_ref.at[b], rates.at[b, :, slot]))
    for b in range(3):
        pairs.append((query_ref.at[b, :, theirs], query_ref.at[b, :, mine], queries.at[b, slot, :]))
    swaps = {}
    locals_ = {}

    def swap(first, last):
        for n in range(first, last):
            away, here, target = pairs[n]
            swaps[n] = push(away, target, swap_send.at[n], swap_recv.at[n], mate)
            swaps[n].start()
            locals_[n] = pltpu.make_async_copy(here, target, local_sem.at[n])
            locals_[n].start()

    def ready(n):
        swaps[n].wait_recv()
        locals_[n].wait()

    def block_of(k, m, p, q):
        return full.at[k, m, p, :, q, core]

    def gather_copy(k, m, n):
        p, q = (
            (pair, lane),
            (pair, lane),
            (1 - pair, lane),
            (pair, lane),
            (1 - pair, lane),
            (pair, 1 - lane),
            (1 - pair, 1 - lane),
        )[n]
        span = block_of(k, m, p, q)
        to = (beyond, beside, beside, partner, partner, partner, partner)[n]
        return push(span, span, gather_send.at[k, m, n], gather_recv.at[k, m, n], to)

    def gather_own(k, m):
        for n in (0, 1, 3):
            go(gather_copy(k, m, n))

    def gather_beyond(k, m):
        gather_copy(k, m, 0).wait_recv()
        go(gather_copy(k, m, 2))
        go(gather_copy(k, m, 4))

    def gather_beside(k, m, n):
        gather_copy(k, m, n).wait_recv()
        go(gather_copy(k, m, n + 4))

    def gather_end(k, m):
        for n in range(3, 7):
            gather_copy(k, m, n).wait_recv()

    def core_copy(t):
        return push(
            core_out.at[t], core_in.at[t], sum_send.at[t, 0], sum_recv.at[t, 0], partner
        )

    def side_copy(t, p, n):
        return push(
            side_out.at[t, p], side_in.at[t, p], sum_send.at[t, n], sum_recv.at[t, n], beside
        )

    def far_copy(t):
        return push(far_out.at[t], far_in.at[t], sum_send.at[t, 3], sum_recv.at[t, 3], beyond)

    def core_start(t):
        core_out[t] = part[t, :, :, :, 1 - core].astype(jnp.bfloat16)
        go(core_copy(t))

    def core_sum(t, p, q):
        return part[t, p, :, q, core] + core_in[t, p, :, q].astype(jnp.float32)

    def side_start(t):
        core_copy(t).wait_recv()
        for n, p in ((1, 1 - pair), (2, pair)):
            side_out[t, p] = core_sum(t, p, 1 - lane).astype(jnp.bfloat16)
            go(side_copy(t, p, n))

    def far_start(t):
        p = 1 - pair
        side_copy(t, p, 1).wait_recv()
        far_out[t] = (core_sum(t, p, lane) + side_in[t, p].astype(jnp.float32)).astype(
            jnp.bfloat16
        )
        go(far_copy(t))

    def total_of(t):
        side_copy(t, pair, 2).wait_recv()
        near = core_sum(t, pair, lane) + side_in[t, pair].astype(jnp.float32)
        far_copy(t).wait_recv()
        return near + far_in[t].astype(jnp.float32)

    order = (2, 0, 1)

    def whole(k, m):
        return full[k, m].reshape(hidden_units, width)

    def forward(k, x):
        gate = dot_nt(x, whole(k, 0))
        up = dot_nt(x, whole(k, 1))
        sig = jax.nn.sigmoid(gate)
        return gate, up, sig, (gate * sig * up).astype(jnp.bfloat16)

    def keys_forward(j):
        gate, up, sig, hidden = forward(0, keys[j])
        gates[...] = gate
        ups[...] = up
        hiddens[...] = hidden

    def steps(j):
        row = jnp.where(head == 0, rates[j, 0:1, :], rates[j, 1:2, :])
        rate = jnp.transpose(jnp.broadcast_to(row, (128, row.shape[1])))[:, 0:1]
        scaled = (rate * values[j].astype(jnp.float32)).astype(jnp.bfloat16)
        part[3 * j + 2] = dot_tn(scaled, hiddens[...]).reshape(part.shape[1:])
        core_start(3 * j + 2)
        back = dot_nn(scaled, whole(0, 2))
        gate = gates[...]
        sig = jax.nn.sigmoid(gate)
        x = keys[j]
        d_gate = (back * ups[...] * sig * (1.0 + gate * (1.0 - sig))).astype(jnp.bfloat16)
        part[3 * j] = dot_tn(d_gate, x).reshape(part.shape[1:])
        core_start(3 * j)
        d_up = (back * gate * sig).astype(jnp.bfloat16)
        part[3 * j + 1] = dot_tn(d_up, x).reshape(part.shape[1:])
        core_start(3 * j + 1)

    outs = []

    def read_hidden(k):
        gate, up, sig, hidden = forward(k, queries[k])
        hiddens[...] = hidden

    def read_out(k):
        result[k] = dot_nt(hiddens[...], whole(k, 2)).astype(jnp.bfloat16)
        away = push(
            result.at[k, other_slot, :],
            out_ref.at[k, :, mine],
            out_send.at[k],
            out_recv.at[k],
            mate,
        )
        away.start()
        here = pltpu.make_async_copy(
            result.at[k, slot, :], out_ref.at[k, :, mine], out_local.at[k]
        )
        here.start()
        outs.append((away, here))

    swap(0, 3)
    for m in range(3):
        ready(m)
        gather_own(0, m)
    swap(3, 9)
    for m in range(3):
        gather_beyond(0, m)
        gather_beside(0, m, 1)
    for m in range(3):
        gather_beside(0, m, 2)
    for m in range(3):
        gather_end(0, m)
    for n in range(3, 6):
        ready(n)
    keys_forward(0)
    steps(0)
    for m in order:
        side_start(m)
    for n in range(6, 9):
        ready(n)
    keys_forward(1)
    steps(1)
    for m in order:
        far_start(m)
        side_start(3 + m)
    swap(9, 10)
    for m in order:
        moment = total_of(m)
        step_own[m] = moment
        old = full[0, m, pair, :, lane, core].astype(jnp.float32)
        fresh = renorm(old, old + moment)
        weight_own[m] = fresh
        full[1, m, pair, :, lane, core] = fresh.astype(jnp.bfloat16)
        gather_own(1, m)
    decay = decay_ref[head]
    for m in order:
        far_start(3 + m)
    swap(10, 11)
    ready(9)
    read_hidden(0)
    read_out(0)
    for m in order:
        gather_beyond(1, m)
        gather_beside(1, m, 1)
    for m in order:
        moment = decay * step_own[m] + total_of(3 + m)
        old = weight_own[m]
        fresh = renorm(old, old + moment)
        full[2, m, pair, :, lane, core] = fresh.astype(jnp.bfloat16)
        gather_own(2, m)
    swap(11, 12)
    for m in order:
        gather_beside(1, m, 2)
    for m in order:
        gather_beyond(2, m)
        gather_beside(2, m, 1)
    for m in range(3):
        gather_end(1, m)
    ready(10)
    read_hidden(1)
    read_out(1)
    ready(11)
    for m in order:
        gather_beside(2, m, 2)
    gather_end(2, 2)
    gather_end(2, 0)
    gates[...] = dot_nt(queries[2], whole(2, 0))
    gather_end(2, 1)
    gate = gates[...]
    up = dot_nt(queries[2], whole(2, 1))
    hiddens[...] = (gate * jax.nn.sigmoid(gate) * up).astype(jnp.bfloat16)
    read_out(2)

    for n in range(len(pairs)):
        swaps[n].wait_send()
    for copy in sent:
        copy.wait_send()
    for away, here in outs:
        here.wait()
        away.wait()


def fused_shards(query, key, value, rate, first, third, second, decay):
    blocks, tokens, features = query.shape
    heads, rows, width = first.shape
    hidden = 16 * rows
    span = 2 * tokens
    anywhere = pl.BlockSpec(memory_space=pl.ANY)
    dma = pltpu.SemaphoreType.DMA
    low, wide = jnp.bfloat16, jnp.float32
    return pl.pallas_call(
        kernel,
        out_shape=jax.ShapeDtypeStruct(query.shape, low),
        in_specs=[anywhere] * 7 + [pl.BlockSpec(memory_space=pltpu.SMEM)],
        out_specs=anywhere,
        scratch_shapes=[
            pltpu.VMEM((3, span, width), low),
            pltpu.VMEM((2, span, width), low),
            pltpu.VMEM((2, span, width), low),
            pltpu.VMEM((2, heads, span), wide),
            pltpu.VMEM((3, 3, 2, 2, 2, 2, rows, width), low),
            pltpu.VMEM((6, 2, 2, 2, 2, rows, width), wide),
            pltpu.VMEM((6, 2, 2, 2, rows, width), low),
            pltpu.VMEM((6, 2, 2, 2, rows, width), low),
            pltpu.VMEM((6, 2, 2, rows, width), low),
            pltpu.VMEM((6, 2, 2, rows, width), low),
            pltpu.VMEM((6, 2, rows, width), low),
            pltpu.VMEM((6, 2, rows, width), low),
            pltpu.VMEM((3, 2, rows, width), wide),
            pltpu.VMEM((3, 2, rows, width), wide),
            pltpu.VMEM((3, span, width), low),
            pltpu.VMEM((span, hidden), wide),
            pltpu.VMEM((span, hidden), wide),
            pltpu.VMEM((span, hidden), low),
            dma((12,)),
            dma((12,)),
            dma((12,)),
            dma((3, 3, 7)),
            dma((3, 3, 7)),
            dma((6, 4)),
            dma((6, 4)),
            dma((3,)),
            dma((3,)),
            dma((3,)),
        ],
        compiler_params=pltpu.CompilerParams(
            collective_id=0, has_side_effects=True, vmem_limit_bytes=60 * 1024 * 1024
        ),
    )(query, key, value, jnp.swapaxes(rate, 1, 2), first, third, second, decay)


def solution(mesh):
    placed = (
        P(None, ("groups", "tok"), None),
        P(None, ("groups", "tok"), None),
        P(None, ("groups", "tok"), None),
        P(None, ("groups", "tok"), None),
        P(None, "tok", None),
        P(None, "tok", None),
        P(None, "tok", None),
        P(),
    )
    chips = mesh.shape["tok"] // 2

    def body(*arrays):
        rows = arrays[4].shape[1]
        if rows % 16 or chips != 8 or arrays[4].shape[0] != 2:
            return shards(*arrays)
        return fused_shards(*arrays)

    return jax.shard_map(
        body,
        mesh=mesh,
        in_specs=placed,
        out_specs=P(None, ("groups", "tok"), None),
        check_vma=False,
    )
```

```python
import jax
import jax.numpy as jnp
from jax import lax
from jax.experimental import pallas as pl
from jax.experimental.pallas import tpu as pltpu
from jax.sharding import PartitionSpec as P

MESH = pl.DeviceIdType.MESH


def forward_parts(weights, inputs):
    first, third, second = weights
    length = inputs.shape[0]
    head_count = first.shape[0]
    shaped = inputs.reshape(length, head_count, -1)
    pre_gate = jnp.einsum("thd,hfd->htf", shaped, first, preferred_element_type=jnp.float32)
    pre_up = jnp.einsum("thd,hfd->htf", shaped, third, preferred_element_type=jnp.float32)
    hidden = (jax.nn.silu(pre_gate) * pre_up).astype(jnp.bfloat16)
    return (shaped, pre_gate, pre_up, hidden)


def apply_block(weights, inputs):
    shaped, pre_gate, pre_up, hidden = forward_parts(weights, inputs)
    result = jnp.einsum("htf,hdf->thd", hidden, weights[2], preferred_element_type=jnp.float32)
    return result.reshape(inputs.shape[0], -1).astype(jnp.bfloat16)


def partial_steps(weights, keys, values, rates):
    shaped, pre_gate, pre_up, hidden = forward_parts(weights, keys)
    length = keys.shape[0]
    head_count = weights[0].shape[0]
    scaled = (
        rates[:, :, None] * values.reshape(length, head_count, -1).astype(jnp.float32)
    ).astype(jnp.bfloat16)
    step_second = jnp.einsum("thd,htf->hdf", scaled, hidden, preferred_element_type=jnp.float32)
    back = jnp.einsum("thd,hdf->htf", scaled, weights[2], preferred_element_type=jnp.float32)
    sig_gate = jax.nn.sigmoid(pre_gate)
    d_gate = (back * pre_up * sig_gate * (1.0 + pre_gate * (1.0 - sig_gate))).astype(jnp.bfloat16)
    d_up = (back * pre_gate * sig_gate).astype(jnp.bfloat16)
    step_first = jnp.einsum("htf,thd->hfd", d_gate, shaped, preferred_element_type=jnp.float32)
    step_third = jnp.einsum("htf,thd->hfd", d_up, shaped, preferred_element_type=jnp.float32)
    return (step_first, step_third, step_second)


def renorm(old, moved):
    old_norm = jnp.sqrt(jnp.sum(old * old, axis=-1, keepdims=True) + 1e-06)
    moved_norm = jnp.sqrt(jnp.sum(moved * moved, axis=-1, keepdims=True) + 1e-06)
    return moved * old_norm / moved_norm


def shards(
    query_tokens,
    key_tokens,
    value_tokens,
    learn_rates,
    fast_first,
    fast_third,
    fast_second,
    momentum_decay,
):
    owned_zero = jnp.stack([fast_first, fast_third, fast_second])
    full_zero = lax.all_gather(owned_zero, "tok", axis=2, tiled=True)
    terms_zero = partial_steps(full_zero, key_tokens[0], value_tokens[0], learn_rates[0])
    terms_one = partial_steps(full_zero, key_tokens[1], value_tokens[1], learn_rates[1])
    step_zero = lax.psum_scatter(
        jnp.stack(terms_zero).astype(jnp.bfloat16), "tok", scatter_dimension=2, tiled=True
    ).astype(jnp.float32)
    step_one = lax.psum_scatter(
        jnp.stack(terms_one).astype(jnp.bfloat16), "tok", scatter_dimension=2, tiled=True
    ).astype(jnp.float32)
    out_zero = apply_block(full_zero, query_tokens[0])
    decay = momentum_decay[None, :, None, None]
    weights_zero = owned_zero.astype(jnp.float32)
    weights_one = renorm(weights_zero, weights_zero + step_zero)
    full_one = lax.all_gather(weights_one.astype(jnp.bfloat16), "tok", axis=2, tiled=True)
    weights_two = renorm(weights_one, weights_one + decay * step_zero + step_one)
    full_two = lax.all_gather(weights_two.astype(jnp.bfloat16), "tok", axis=2, tiled=True)
    out_one = apply_block(full_one, query_tokens[1])
    out_two = apply_block(full_two, query_tokens[2])
    return jnp.stack([out_zero, out_one, out_two])


def dot_nt(a, b):
    return lax.dot_general(a, b, (((1,), (1,)), ((), ())), preferred_element_type=jnp.float32)


def dot_nn(a, b):
    return lax.dot_general(a, b, (((1,), (0,)), ((), ())), preferred_element_type=jnp.float32)


def dot_tn(a, b):
    return lax.dot_general(a, b, (((0,), (0,)), ((), ())), preferred_element_type=jnp.float32)


def kernel(
    query_ref,
    key_ref,
    value_ref,
    rate_ref,
    first_ref,
    third_ref,
    second_ref,
    decay_ref,
    out_ref,
    queries,
    keys,
    values,
    rates,
    full,
    part,
    core_out,
    core_in,
    side_out,
    side_in,
    far_out,
    far_in,
    step_own,
    weight_own,
    result,
    gates,
    ups,
    hiddens,
    swap_send,
    swap_recv,
    local_sem,
    gather_send,
    gather_recv,
    sum_send,
    sum_recv,
    out_send,
    out_recv,
    out_local,
):
    index = lax.axis_index("tok")
    core = index % 2
    lane = (index // 2) % 2
    head = (index // 4) % 2
    pair = index // 8
    partner = {"tok": index + 1 - 2 * core}
    beside = {"tok": index + 2 - 4 * lane}
    mate = {"tok": index + 4 - 8 * head}
    beyond = {"tok": index + 8 - 16 * pair}
    rows = first_ref.shape[1]
    tokens = key_ref.shape[1]
    width = first_ref.shape[2]
    hidden_units = 16 * rows

    barrier = pltpu.get_barrier_semaphore()
    for other in (partner, beside, mate, beyond):
        pl.semaphore_signal(barrier, inc=1, device_id=other, device_id_type=MESH)
    pl.semaphore_wait(barrier, 4)

    sent = []

    def push(src, dst, send_sem, recv_sem, to):
        return pltpu.make_async_remote_copy(
            src_ref=src,
            dst_ref=dst,
            send_sem=send_sem,
            recv_sem=recv_sem,
            device_id=to,
            device_id_type=MESH,
        )

    def go(copy):
        copy.start()
        sent.append(copy)

    mine = pl.ds(pl.multiple_of(head * width, width), width)
    theirs = pl.ds(pl.multiple_of((1 - head) * width, width), width)
    slot = pl.ds(pl.multiple_of(head * tokens, tokens), tokens)
    other_slot = pl.ds(pl.multiple_of((1 - head) * tokens, tokens), tokens)

    pairs = []
    for m, ref in enumerate((first_ref, third_ref, second_ref)):
        pairs.append((ref.at[1 - head], ref.at[head], full.at[0, m, pair, head, lane, core]))
    for b in range(2):
        pairs.append((key_ref.at[b, :, theirs], key_ref.at[b, :, mine], keys.at[b, slot, :]))
        pairs.append((value_ref.at[b, :, theirs], value_ref.at[b, :, mine], values.at[b, slot, :]))
        pairs.append((rate_ref.at[b], rate_ref.at[b], rates.at[b, :, slot]))
    for b in range(3):
        pairs.append((query_ref.at[b, :, theirs], query_ref.at[b, :, mine], queries.at[b, slot, :]))
    swaps = {}
    locals_ = {}

    def swap(first, last):
        for n in range(first, last):
            away, here, target = pairs[n]
            swaps[n] = push(away, target, swap_send.at[n], swap_recv.at[n], mate)
            swaps[n].start()
            locals_[n] = pltpu.make_async_copy(here, target, local_sem.at[n])
            locals_[n].start()

    def ready(n):
        swaps[n].wait_recv()
        locals_[n].wait()

    def block_of(k, m, p, q):
        return full.at[k, m, p, :, q, core]

    def gather_copy(k, m, n, u=None):
        p, q = (
            (pair, lane),
            (pair, lane),
            (1 - pair, lane),
            (pair, lane),
            (1 - pair, lane),
            (pair, 1 - lane),
            (1 - pair, 1 - lane),
        )[n]
        if u is None:
            span, j = block_of(k, m, p, q), m
        else:
            owner = head if u == 0 else 1 - head
            span, j = full.at[k, m, p, owner, q, core], 2 * m + u
        to = (beyond, beside, beside, partner, partner, partner, partner)[n]
        return push(span, span, gather_send.at[k, j, n], gather_recv.at[k, j, n], to)

    def gather_own(k, m, u=None):
        for n in (0, 1, 3):
            go(gather_copy(k, m, n, u))

    def gather_beyond(k, m, u=None):
        gather_copy(k, m, 0, u).wait_recv()
        go(gather_copy(k, m, 2, u))
        go(gather_copy(k, m, 4, u))

    def gather_beside(k, m, n, u=None):
        gather_copy(k, m, n, u).wait_recv()
        go(gather_copy(k, m, n + 4, u))

    def gather_end(k, m, u=None):
        for n in range(3, 7):
            gather_copy(k, m, n, u).wait_recv()

    def core_copy(t):
        return push(
            core_out.at[t], core_in.at[t], sum_send.at[t, 0], sum_recv.at[t, 0], partner
        )

    def side_copy(t, p, n):
        return push(
            side_out.at[t, p], side_in.at[t, p], sum_send.at[t, n], sum_recv.at[t, n], beside
        )

    def far_copy(t):
        return push(far_out.at[t], far_in.at[t], sum_send.at[t, 3], sum_recv.at[t, 3], beyond)

    def core_start(t):
        core_out[t] = part[t, :, :, :, 1 - core].astype(jnp.bfloat16)
        go(core_copy(t))

    def core_sum(t, p, q):
        return part[t, p, :, q, core] + core_in[t, p, :, q].astype(jnp.float32)

    def side_start(t):
        core_copy(t).wait_recv()
        for n, p in ((1, 1 - pair), (2, pair)):
            side_out[t, p] = core_sum(t, p, 1 - lane).astype(jnp.bfloat16)
            go(side_copy(t, p, n))

    def far_start(t):
        p = 1 - pair
        side_copy(t, p, 1).wait_recv()
        far_out[t] = (core_sum(t, p, lane) + side_in[t, p].astype(jnp.float32)).astype(
            jnp.bfloat16
        )
        go(far_copy(t))

    def total_of(t):
        side_copy(t, pair, 2).wait_recv()
        near = core_sum(t, pair, lane) + side_in[t, pair].astype(jnp.float32)
        far_copy(t).wait_recv()
        return near + far_in[t].astype(jnp.float32)

    order = (2, 0, 1)

    def whole(k, m):
        return full[k, m].reshape(hidden_units, width)

    def forward(k, x):
        gate = dot_nt(x, whole(k, 0))
        up = dot_nt(x, whole(k, 1))
        sig = jax.nn.sigmoid(gate)
        return gate, up, sig, (gate * sig * up).astype(jnp.bfloat16)

    def keys_forward(j):
        gate, up, sig, hidden = forward(0, keys[j])
        gates[...] = gate
        ups[...] = up
        hiddens[...] = hidden

    def steps(j):
        row = jnp.where(head == 0, rates[j, 0:1, :], rates[j, 1:2, :])
        rate = jnp.transpose(jnp.broadcast_to(row, (128, row.shape[1])))[:, 0:1]
        scaled = (rate * values[j].astype(jnp.float32)).astype(jnp.bfloat16)
        part[3 * j + 2] = dot_tn(scaled, hiddens[...]).reshape(part.shape[1:])
        core_start(3 * j + 2)
        back = dot_nn(scaled, whole(0, 2))
        gate = gates[...]
        sig = jax.nn.sigmoid(gate)
        x = keys[j]
        d_gate = (back * ups[...] * sig * (1.0 + gate * (1.0 - sig))).astype(jnp.bfloat16)
        part[3 * j] = dot_tn(d_gate, x).reshape(part.shape[1:])
        core_start(3 * j)
        d_up = (back * gate * sig).astype(jnp.bfloat16)
        part[3 * j + 1] = dot_tn(d_up, x).reshape(part.shape[1:])
        core_start(3 * j + 1)

    outs = []

    def read_hidden(k):
        gate, up, sig, hidden = forward(k, queries[k])
        hiddens[...] = hidden

    def read_out(k):
        second = whole(k, 2)
        result[k, other_slot, :] = dot_nt(hiddens[other_slot, :], second).astype(jnp.bfloat16)
        away = push(
            result.at[k, other_slot, :],
            out_ref.at[k, :, mine],
            out_send.at[k],
            out_recv.at[k],
            mate,
        )
        away.start()
        result[k, slot, :] = dot_nt(hiddens[slot, :], second).astype(jnp.bfloat16)
        here = pltpu.make_async_copy(
            result.at[k, slot, :], out_ref.at[k, :, mine], out_local.at[k]
        )
        here.start()
        outs.append((away, here))

    swap(0, 3)
    for m in range(3):
        locals_[m].wait()
        gather_own(0, m, 0)
    for m in range(3):
        swaps[m].wait_recv()
        gather_own(0, m, 1)
    swap(3, 9)
    for u in range(2):
        for m in range(3):
            gather_beyond(0, m, u)
            gather_beside(0, m, 1, u)
    for u in range(2):
        for m in range(3):
            gather_beside(0, m, 2, u)
    for u in range(2):
        for m in range(3):
            gather_end(0, m, u)
    for n in range(3, 6):
        ready(n)
    keys_forward(0)
    steps(0)
    for m in order:
        side_start(m)
    for n in range(6, 9):
        ready(n)
    keys_forward(1)
    steps(1)
    for m in order:
        far_start(m)
        side_start(3 + m)
    swap(9, 10)
    for m in order:
        moment = total_of(m)
        step_own[m] = moment
        old = full[0, m, pair, :, lane, core].astype(jnp.float32)
        fresh = renorm(old, old + moment)
        weight_own[m] = fresh
        full[1, m, pair, :, lane, core] = fresh.astype(jnp.bfloat16)
        gather_own(1, m)
    decay = decay_ref[head]
    for m in order:
        far_start(3 + m)
    swap(10, 11)
    ready(9)
    read_hidden(0)
    read_out(0)
    for m in order:
        gather_beyond(1, m)
        gather_beside(1, m, 1)
    for m in order:
        moment = decay * step_own[m] + total_of(3 + m)
        old = weight_own[m]
        fresh = renorm(old, old + moment)
        full[2, m, pair, :, lane, core] = fresh.astype(jnp.bfloat16)
        gather_own(2, m)
    swap(11, 12)
    for m in order:
        gather_beside(1, m, 2)
    for m in order:
        gather_beyond(2, m)
        gather_beside(2, m, 1)
    for m in range(3):
        gather_end(1, m)
    ready(10)
    read_hidden(1)
    read_out(1)
    ready(11)
    for m in order:
        gather_beside(2, m, 2)
    gather_end(2, 2)
    gather_end(2, 0)
    gates[...] = dot_nt(queries[2], whole(2, 0))
    gather_end(2, 1)
    gate = gates[...]
    up = dot_nt(queries[2], whole(2, 1))
    hiddens[...] = (gate * jax.nn.sigmoid(gate) * up).astype(jnp.bfloat16)
    read_out(2)

    for n in range(len(pairs)):
        swaps[n].wait_send()
    for copy in sent:
        copy.wait_send()
    for away, here in outs:
        here.wait()
        away.wait()


def fused_shards(query, key, value, rate, first, third, second, decay):
    blocks, tokens, features = query.shape
    heads, rows, width = first.shape
    hidden = 16 * rows
    span = 2 * tokens
    anywhere = pl.BlockSpec(memory_space=pl.ANY)
    dma = pltpu.SemaphoreType.DMA
    low, wide = jnp.bfloat16, jnp.float32
    return pl.pallas_call(
        kernel,
        out_shape=jax.ShapeDtypeStruct(query.shape, low),
        in_specs=[anywhere] * 7 + [pl.BlockSpec(memory_space=pltpu.SMEM)],
        out_specs=anywhere,
        scratch_shapes=[
            pltpu.VMEM((3, span, width), low),
            pltpu.VMEM((2, span, width), low),
            pltpu.VMEM((2, span, width), low),
            pltpu.VMEM((2, heads, span), wide),
            pltpu.VMEM((3, 3, 2, 2, 2, 2, rows, width), low),
            pltpu.VMEM((6, 2, 2, 2, 2, rows, width), wide),
            pltpu.VMEM((6, 2, 2, 2, rows, width), low),
            pltpu.VMEM((6, 2, 2, 2, rows, width), low),
            pltpu.VMEM((6, 2, 2, rows, width), low),
            pltpu.VMEM((6, 2, 2, rows, width), low),
            pltpu.VMEM((6, 2, rows, width), low),
            pltpu.VMEM((6, 2, rows, width), low),
            pltpu.VMEM((3, 2, rows, width), wide),
            pltpu.VMEM((3, 2, rows, width), wide),
            pltpu.VMEM((3, span, width), low),
            pltpu.VMEM((span, hidden), wide),
            pltpu.VMEM((span, hidden), wide),
            pltpu.VMEM((span, hidden), low),
            dma((12,)),
            dma((12,)),
            dma((12,)),
            dma((3, 6, 7)),
            dma((3, 6, 7)),
            dma((6, 4)),
            dma((6, 4)),
            dma((3,)),
            dma((3,)),
            dma((3,)),
        ],
        compiler_params=pltpu.CompilerParams(
            collective_id=0, has_side_effects=True, vmem_limit_bytes=60 * 1024 * 1024
        ),
    )(query, key, value, jnp.swapaxes(rate, 1, 2), first, third, second, decay)


def solution(mesh):
    placed = (
        P(None, ("groups", "tok"), None),
        P(None, ("groups", "tok"), None),
        P(None, ("groups", "tok"), None),
        P(None, ("groups", "tok"), None),
        P(None, "tok", None),
        P(None, "tok", None),
        P(None, "tok", None),
        P(),
    )
    chips = mesh.shape["tok"] // 2

    def body(*arrays):
        rows = arrays[4].shape[1]
        if rows % 16 or chips != 8 or arrays[4].shape[0] != 2:
            return shards(*arrays)
        return fused_shards(*arrays)

    return jax.shard_map(
        body,
        mesh=mesh,
        in_specs=placed,
        out_specs=P(None, ("groups", "tok"), None),
        check_vma=False,
    )
```

```python
import jax
import jax.numpy as jnp
from jax import lax
from jax.experimental import pallas as pl
from jax.experimental.pallas import tpu as pltpu
from jax.sharding import PartitionSpec as P

MESH = pl.DeviceIdType.MESH


def forward_parts(weights, inputs):
    first, third, second = weights
    length = inputs.shape[0]
    head_count = first.shape[0]
    shaped = inputs.reshape(length, head_count, -1)
    pre_gate = jnp.einsum("thd,hfd->htf", shaped, first, preferred_element_type=jnp.float32)
    pre_up = jnp.einsum("thd,hfd->htf", shaped, third, preferred_element_type=jnp.float32)
    hidden = (jax.nn.silu(pre_gate) * pre_up).astype(jnp.bfloat16)
    return (shaped, pre_gate, pre_up, hidden)


def apply_block(weights, inputs):
    shaped, pre_gate, pre_up, hidden = forward_parts(weights, inputs)
    result = jnp.einsum("htf,hdf->thd", hidden, weights[2], preferred_element_type=jnp.float32)
    return result.reshape(inputs.shape[0], -1).astype(jnp.bfloat16)


def partial_steps(weights, keys, values, rates):
    shaped, pre_gate, pre_up, hidden = forward_parts(weights, keys)
    length = keys.shape[0]
    head_count = weights[0].shape[0]
    scaled = (
        rates[:, :, None] * values.reshape(length, head_count, -1).astype(jnp.float32)
    ).astype(jnp.bfloat16)
    step_second = jnp.einsum("thd,htf->hdf", scaled, hidden, preferred_element_type=jnp.float32)
    back = jnp.einsum("thd,hdf->htf", scaled, weights[2], preferred_element_type=jnp.float32)
    sig_gate = jax.nn.sigmoid(pre_gate)
    d_gate = (back * pre_up * sig_gate * (1.0 + pre_gate * (1.0 - sig_gate))).astype(jnp.bfloat16)
    d_up = (back * pre_gate * sig_gate).astype(jnp.bfloat16)
    step_first = jnp.einsum("htf,thd->hfd", d_gate, shaped, preferred_element_type=jnp.float32)
    step_third = jnp.einsum("htf,thd->hfd", d_up, shaped, preferred_element_type=jnp.float32)
    return (step_first, step_third, step_second)


def renorm(old, moved):
    old_norm = jnp.sqrt(jnp.sum(old * old, axis=-1, keepdims=True) + 1e-06)
    moved_norm = jnp.sqrt(jnp.sum(moved * moved, axis=-1, keepdims=True) + 1e-06)
    return moved * old_norm / moved_norm


def shards(
    query_tokens,
    key_tokens,
    value_tokens,
    learn_rates,
    fast_first,
    fast_third,
    fast_second,
    momentum_decay,
):
    owned_zero = jnp.stack([fast_first, fast_third, fast_second])
    full_zero = lax.all_gather(owned_zero, "tok", axis=2, tiled=True)
    terms_zero = partial_steps(full_zero, key_tokens[0], value_tokens[0], learn_rates[0])
    terms_one = partial_steps(full_zero, key_tokens[1], value_tokens[1], learn_rates[1])
    step_zero = lax.psum_scatter(
        jnp.stack(terms_zero).astype(jnp.bfloat16), "tok", scatter_dimension=2, tiled=True
    ).astype(jnp.float32)
    step_one = lax.psum_scatter(
        jnp.stack(terms_one).astype(jnp.bfloat16), "tok", scatter_dimension=2, tiled=True
    ).astype(jnp.float32)
    out_zero = apply_block(full_zero, query_tokens[0])
    decay = momentum_decay[None, :, None, None]
    weights_zero = owned_zero.astype(jnp.float32)
    weights_one = renorm(weights_zero, weights_zero + step_zero)
    full_one = lax.all_gather(weights_one.astype(jnp.bfloat16), "tok", axis=2, tiled=True)
    weights_two = renorm(weights_one, weights_one + decay * step_zero + step_one)
    full_two = lax.all_gather(weights_two.astype(jnp.bfloat16), "tok", axis=2, tiled=True)
    out_one = apply_block(full_one, query_tokens[1])
    out_two = apply_block(full_two, query_tokens[2])
    return jnp.stack([out_zero, out_one, out_two])


def dot_nt(a, b):
    return lax.dot_general(a, b, (((1,), (1,)), ((), ())), preferred_element_type=jnp.float32)


def dot_nn(a, b):
    return lax.dot_general(a, b, (((1,), (0,)), ((), ())), preferred_element_type=jnp.float32)


def dot_tn(a, b):
    return lax.dot_general(a, b, (((0,), (0,)), ((), ())), preferred_element_type=jnp.float32)


def kernel(
    query_ref,
    key_ref,
    value_ref,
    rate_ref,
    first_ref,
    third_ref,
    second_ref,
    decay_ref,
    out_ref,
    queries,
    keys,
    values,
    rates,
    full,
    part,
    core_out,
    core_in,
    side_out,
    side_in,
    far_out,
    far_in,
    step_own,
    weight_own,
    result,
    gates,
    ups,
    hiddens,
    swap_send,
    swap_recv,
    local_sem,
    gather_send,
    gather_recv,
    share_send,
    share_recv,
    sum_send,
    sum_recv,
    out_send,
    out_recv,
    out_local,
):
    index = lax.axis_index("tok")
    core = index % 2
    lane = (index // 2) % 2
    head = (index // 4) % 2
    pair = index // 8
    group = lax.axis_index("groups")
    across = {"groups": 1 - group}
    partner = {"tok": index + 1 - 2 * core}
    beside = {"tok": index + 2 - 4 * lane}
    mate = {"tok": index + 4 - 8 * head}
    beyond = {"tok": index + 8 - 16 * pair}
    rows = first_ref.shape[1]
    tokens = key_ref.shape[1]
    width = first_ref.shape[2]
    hidden_units = 16 * rows

    barrier = pltpu.get_barrier_semaphore()
    for other in (partner, beside, mate, beyond, across):
        pl.semaphore_signal(barrier, inc=1, device_id=other, device_id_type=MESH)
    pl.semaphore_wait(barrier, 5)

    sent = []

    def push(src, dst, send_sem, recv_sem, to):
        return pltpu.make_async_remote_copy(
            src_ref=src,
            dst_ref=dst,
            send_sem=send_sem,
            recv_sem=recv_sem,
            device_id=to,
            device_id_type=MESH,
        )

    def go(copy):
        copy.start()
        sent.append(copy)

    mine = pl.ds(pl.multiple_of(head * width, width), width)
    theirs = pl.ds(pl.multiple_of((1 - head) * width, width), width)
    slot = pl.ds(pl.multiple_of(head * tokens, tokens), tokens)
    other_slot = pl.ds(pl.multiple_of((1 - head) * tokens, tokens), tokens)

    pairs = []
    for m, ref in enumerate((first_ref, third_ref, second_ref)):
        pairs.append((ref.at[1 - head], ref.at[head], full.at[0, m, pair, head, lane, core]))
    for b in range(2):
        pairs.append((key_ref.at[b, :, theirs], key_ref.at[b, :, mine], keys.at[b, slot, :]))
        pairs.append((value_ref.at[b, :, theirs], value_ref.at[b, :, mine], values.at[b, slot, :]))
        pairs.append((rate_ref.at[b], rate_ref.at[b], rates.at[b, :, slot]))
    for b in range(3):
        pairs.append((query_ref.at[b, :, theirs], query_ref.at[b, :, mine], queries.at[b, slot, :]))
    swaps = {}
    locals_ = {}

    def swap(first, last):
        for n in range(first, last):
            away, here, target = pairs[n]
            swaps[n] = push(away, target, swap_send.at[n], swap_recv.at[n], mate)
            swaps[n].start()
            locals_[n] = pltpu.make_async_copy(here, target, local_sem.at[n])
            locals_[n].start()

    def ready(n):
        swaps[n].wait_recv()
        locals_[n].wait()

    def block_of(k, m, p, q):
        return full.at[k, m, p, :, q, core]

    def gather_copy(k, m, n):
        p, q = (
            (pair, lane),
            (pair, lane),
            (1 - pair, lane),
            (pair, lane),
            (1 - pair, lane),
            (pair, 1 - lane),
            (1 - pair, 1 - lane),
        )[n]
        span = block_of(k, m, p, q)
        to = (beyond, beside, beside, partner, partner, partner, partner)[n]
        return push(span, span, gather_send.at[k, m, n], gather_recv.at[k, m, n], to)

    share = pl.ds(pl.multiple_of(group * (width // 2), width // 2), width // 2)

    def share_copy(m, n):
        copy_from, to = (
            ((pair, lane), beyond),
            ((pair, lane), beside),
            ((1 - pair, lane), beside),
            ((1 - pair, lane), across),
            ((pair, 1 - lane), across),
            ((1 - pair, 1 - lane), across),
        )[n]
        span = full.at[0, m, copy_from[0], :, copy_from[1], core, :, share]
        return push(span, span, share_send.at[m, n], share_recv.at[m, n], to)

    def share_all():
        for m in range(3):
            share_copy(m, 0).wait_recv()
            go(share_copy(m, 2))
            go(share_copy(m, 3))
            share_copy(m, 1).wait_recv()
            go(share_copy(m, 4))
        for m in range(3):
            share_copy(m, 3).wait_recv()
            go(gather_copy(0, m, 4))
            share_copy(m, 2).wait_recv()
            go(share_copy(m, 5))
            share_copy(m, 4).wait_recv()
            go(gather_copy(0, m, 5))
        for m in range(3):
            share_copy(m, 5).wait_recv()
            go(gather_copy(0, m, 6))

    def gather_own(k, m):
        for n in (0, 1, 3):
            go(gather_copy(k, m, n))

    def gather_beyond(k, m):
        gather_copy(k, m, 0).wait_recv()
        go(gather_copy(k, m, 2))
        go(gather_copy(k, m, 4))

    def gather_beside(k, m, n):
        gather_copy(k, m, n).wait_recv()
        go(gather_copy(k, m, n + 4))

    def gather_end(k, m):
        for n in range(3, 7):
            gather_copy(k, m, n).wait_recv()

    def core_copy(t):
        return push(
            core_out.at[t], core_in.at[t], sum_send.at[t, 0], sum_recv.at[t, 0], partner
        )

    def side_copy(t, p, n):
        return push(
            side_out.at[t, p], side_in.at[t, p], sum_send.at[t, n], sum_recv.at[t, n], beside
        )

    def far_copy(t):
        return push(far_out.at[t], far_in.at[t], sum_send.at[t, 3], sum_recv.at[t, 3], beyond)

    def core_start(t):
        core_out[t] = part[t, :, :, :, 1 - core].astype(jnp.bfloat16)
        go(core_copy(t))

    def core_sum(t, p, q):
        return part[t, p, :, q, core] + core_in[t, p, :, q].astype(jnp.float32)

    def side_start(t):
        core_copy(t).wait_recv()
        for n, p in ((1, 1 - pair), (2, pair)):
            side_out[t, p] = core_sum(t, p, 1 - lane).astype(jnp.bfloat16)
            go(side_copy(t, p, n))

    def far_start(t):
        p = 1 - pair
        side_copy(t, p, 1).wait_recv()
        far_out[t] = (core_sum(t, p, lane) + side_in[t, p].astype(jnp.float32)).astype(
            jnp.bfloat16
        )
        go(far_copy(t))

    def total_of(t):
        side_copy(t, pair, 2).wait_recv()
        near = core_sum(t, pair, lane) + side_in[t, pair].astype(jnp.float32)
        far_copy(t).wait_recv()
        return near + far_in[t].astype(jnp.float32)

    order = (2, 0, 1)

    def whole(k, m):
        return full[k, m].reshape(hidden_units, width)

    def forward(k, x):
        gate = dot_nt(x, whole(k, 0))
        up = dot_nt(x, whole(k, 1))
        sig = jax.nn.sigmoid(gate)
        return gate, up, sig, (gate * sig * up).astype(jnp.bfloat16)

    def keys_forward(j):
        gate, up, sig, hidden = forward(0, keys[j])
        gates[...] = gate
        ups[...] = up
        hiddens[...] = hidden

    def steps(j):
        row = jnp.where(head == 0, rates[j, 0:1, :], rates[j, 1:2, :])
        rate = jnp.transpose(jnp.broadcast_to(row, (128, row.shape[1])))[:, 0:1]
        scaled = (rate * values[j].astype(jnp.float32)).astype(jnp.bfloat16)
        part[3 * j + 2] = dot_tn(scaled, hiddens[...]).reshape(part.shape[1:])
        core_start(3 * j + 2)
        back = dot_nn(scaled, whole(0, 2))
        gate = gates[...]
        sig = jax.nn.sigmoid(gate)
        x = keys[j]
        d_gate = (back * ups[...] * sig * (1.0 + gate * (1.0 - sig))).astype(jnp.bfloat16)
        part[3 * j] = dot_tn(d_gate, x).reshape(part.shape[1:])
        core_start(3 * j)
        d_up = (back * gate * sig).astype(jnp.bfloat16)
        part[3 * j + 1] = dot_tn(d_up, x).reshape(part.shape[1:])
        core_start(3 * j + 1)

    outs = []

    def read_hidden(k):
        gate, up, sig, hidden = forward(k, queries[k])
        hiddens[...] = hidden

    def read_out(k):
        result[k] = dot_nt(hiddens[...], whole(k, 2)).astype(jnp.bfloat16)
        away = push(
            result.at[k, other_slot, :],
            out_ref.at[k, :, mine],
            out_send.at[k],
            out_recv.at[k],
            mate,
        )
        away.start()
        here = pltpu.make_async_copy(
            result.at[k, slot, :], out_ref.at[k, :, mine], out_local.at[k]
        )
        here.start()
        outs.append((away, here))

    swap(0, 3)
    for m in range(3):
        ready(m)
        go(share_copy(m, 0))
        go(share_copy(m, 1))
        go(gather_copy(0, m, 3))
    swap(3, 9)
    share_all()
    for m in range(3):
        gather_end(0, m)
    for n in range(3, 6):
        ready(n)
    keys_forward(0)
    steps(0)
    for m in order:
        side_start(m)
    for n in range(6, 9):
        ready(n)
    keys_forward(1)
    steps(1)
    for m in order:
        far_start(m)
        side_start(3 + m)
    swap(9, 10)
    for m in order:
        moment = total_of(m)
        step_own[m] = moment
        old = full[0, m, pair, :, lane, core].astype(jnp.float32)
        fresh = renorm(old, old + moment)
        weight_own[m] = fresh
        full[1, m, pair, :, lane, core] = fresh.astype(jnp.bfloat16)
        gather_own(1, m)
    decay = decay_ref[head]
    for m in order:
        far_start(3 + m)
    swap(10, 11)
    ready(9)
    read_hidden(0)
    read_out(0)
    for m in order:
        gather_beyond(1, m)
        gather_beside(1, m, 1)
    for m in order:
        moment = decay * step_own[m] + total_of(3 + m)
        old = weight_own[m]
        fresh = renorm(old, old + moment)
        full[2, m, pair, :, lane, core] = fresh.astype(jnp.bfloat16)
        gather_own(2, m)
    swap(11, 12)
    for m in order:
        gather_beside(1, m, 2)
    for m in order:
        gather_beyond(2, m)
        gather_beside(2, m, 1)
    for m in range(3):
        gather_end(1, m)
    ready(10)
    read_hidden(1)
    read_out(1)
    ready(11)
    for m in order:
        gather_beside(2, m, 2)
    gather_end(2, 2)
    gather_end(2, 0)
    gates[...] = dot_nt(queries[2], whole(2, 0))
    gather_end(2, 1)
    gate = gates[...]
    up = dot_nt(queries[2], whole(2, 1))
    hiddens[...] = (gate * jax.nn.sigmoid(gate) * up).astype(jnp.bfloat16)
    read_out(2)

    for n in range(len(pairs)):
        swaps[n].wait_send()
    for copy in sent:
        copy.wait_send()
    for away, here in outs:
        here.wait()
        away.wait()


def fused_shards(query, key, value, rate, first, third, second, decay):
    blocks, tokens, features = query.shape
    heads, rows, width = first.shape
    hidden = 16 * rows
    span = 2 * tokens
    anywhere = pl.BlockSpec(memory_space=pl.ANY)
    dma = pltpu.SemaphoreType.DMA
    low, wide = jnp.bfloat16, jnp.float32
    return pl.pallas_call(
        kernel,
        out_shape=jax.ShapeDtypeStruct(query.shape, low),
        in_specs=[anywhere] * 7 + [pl.BlockSpec(memory_space=pltpu.SMEM)],
        out_specs=anywhere,
        scratch_shapes=[
            pltpu.VMEM((3, span, width), low),
            pltpu.VMEM((2, span, width), low),
            pltpu.VMEM((2, span, width), low),
            pltpu.VMEM((2, heads, span), wide),
            pltpu.VMEM((3, 3, 2, 2, 2, 2, rows, width), low),
            pltpu.VMEM((6, 2, 2, 2, 2, rows, width), wide),
            pltpu.VMEM((6, 2, 2, 2, rows, width), low),
            pltpu.VMEM((6, 2, 2, 2, rows, width), low),
            pltpu.VMEM((6, 2, 2, rows, width), low),
            pltpu.VMEM((6, 2, 2, rows, width), low),
            pltpu.VMEM((6, 2, rows, width), low),
            pltpu.VMEM((6, 2, rows, width), low),
            pltpu.VMEM((3, 2, rows, width), wide),
            pltpu.VMEM((3, 2, rows, width), wide),
            pltpu.VMEM((3, span, width), low),
            pltpu.VMEM((span, hidden), wide),
            pltpu.VMEM((span, hidden), wide),
            pltpu.VMEM((span, hidden), low),
            dma((12,)),
            dma((12,)),
            dma((12,)),
            dma((3, 3, 7)),
            dma((3, 3, 7)),
            dma((3, 6)),
            dma((3, 6)),
            dma((6, 4)),
            dma((6, 4)),
            dma((3,)),
            dma((3,)),
            dma((3,)),
        ],
        compiler_params=pltpu.CompilerParams(
            collective_id=0, has_side_effects=True, vmem_limit_bytes=60 * 1024 * 1024
        ),
    )(query, key, value, jnp.swapaxes(rate, 1, 2), first, third, second, decay)


def solution(mesh):
    placed = (
        P(None, ("groups", "tok"), None),
        P(None, ("groups", "tok"), None),
        P(None, ("groups", "tok"), None),
        P(None, ("groups", "tok"), None),
        P(None, "tok", None),
        P(None, "tok", None),
        P(None, "tok", None),
        P(),
    )
    chips = mesh.shape["tok"] // 2

    def body(*arrays):
        rows = arrays[4].shape[1]
        if rows % 16 or chips != 8 or arrays[4].shape[0] != 2 or mesh.shape["groups"] != 2:
            return shards(*arrays)
        return fused_shards(*arrays)

    return jax.shard_map(
        body,
        mesh=mesh,
        in_specs=placed,
        out_specs=P(None, ("groups", "tok"), None),
        check_vma=False,
    )
```
